32 devices in a mesh: chan: 4 (over y, x), panel: 8 (over z, core).
Axes of the slice: x: 2, y: 2, z: 4, core: 2. Of those that a mesh axis runs over, the one named last changes fastest.
Arguments:
- voltages: bfloat16 [512, 536576], P(('chan', 'panel')), may hold values from -6 to 6
- prototype: float32 [4, 4096], replicated, may hold values from -0.046875 to 0.046875
- complex_gains: float32 [512, 48], P(('chan', 'panel')), may hold values from -4 to 4
- flagged: int32 [256], P(('chan', 'panel')), may hold values 0 or 1
- station_order: int32 [256], replicated, may hold values from 0 to 255, each once
Outputs:
- visibilities: bfloat16 [2, 24, 512, 512], P(None, 'chan', 'panel')
The draws below stay inside these ranges and needn't reach their ends.
Inputs may be any that keep to these rules, and one draw needn't show every extreme that they name: `station_order`: each station appears once.
All inputs are finite; a program needn't handle non-finite values. No bound on the sum of `flagged` on one device may be relied on, other than what follows from the above.
Results may differ from the reference program's by a relative error of at most 0.0073.
Values may be sent and summed in bfloat16 or wider, within the bound.
No kernel may reach another device: no remote copies, remote signals or barrier semaphores. Data moves between devices by JAX's collectives and lax.ppermute only.
A program may use at most 128 MiB of HBM per device.

```python
import math
import jax
import jax.numpy as jnp
from jax import lax

NFFT = 4096
TAPS = 4
STA_DEV = 8
FRAMES = 128
STATIONS = 256
INPUTS = 512
NCHAN = 24


def touch_ends(entries, key, low, largest):
    extent = entries.shape
    index_at = [jax.random.randint(jax.random.fold_in(key, axis), (), 0, extent[axis]) for axis in range(len(extent))]
    entries = entries.at[tuple(index_at)].set(low)
    longest = extent.index(max(extent))
    index_at[longest] = (index_at[longest] + 1) % extent[longest]
    return entries.at[tuple(index_at)].set(largest)


def level_of(own_key, extent, cuts, least, top_value):
    def one(axis_at, blocks):
        heights = jax.random.uniform(jax.random.fold_in(jax.random.fold_in(own_key, 6), axis_at), (blocks,), jnp.float32, least / len(cuts), top_value / len(cuts))
        return jnp.repeat(jnp.exp(heights), extent[axis_at] // blocks).reshape((-1,) + (1,) * (len(extent) - axis_at - 1))

    level = one(*cuts[0])
    for cut in cuts[1:]:
        level = level * one(*cut)
    return level


def scatter_about(own_key, dims, spread, reach, cuts=(), kind=jnp.bfloat16):
    entries = jax.random.normal(own_key, dims, jnp.float32) * spread
    if len(cuts) > 0:
        entries = level_of(own_key, dims, cuts, -0.22, 0.18) * entries
    return jnp.clip(entries, min=-reach, max=reach).astype(kind)


def setup_inputs(seed: int = 0) -> dict:
    streams_of = jax.random.split(jax.random.key(seed), 6)
    voltages = scatter_about(streams_of[0], (INPUTS, (FRAMES + TAPS - 1) * NFFT), 1.0, 6.0, ((0, 32),))
    prototype = scatter_about(streams_of[1], (TAPS, NFFT), (TAPS * NFFT) ** -0.5, 0.046875, (), jnp.float32)
    complex_gains = scatter_about(streams_of[2], (INPUTS, 2 * NCHAN), 0.7, 4.0, ((0, 32),), jnp.float32)
    flagged = touch_ends((jax.random.randint(streams_of[3], (STATIONS,), 0, 8) < 1).astype(jnp.int32), jax.random.fold_in(streams_of[3], 1), 0, 1)
    station_order = jax.random.permutation(streams_of[4], STATIONS).astype(jnp.int32)
    return dict(voltages=voltages, prototype=prototype, complex_gains=complex_gains, flagged=flagged, station_order=station_order)


def make_table(length, channels):
    sample = jnp.arange(length, dtype=jnp.int32)[:, None]
    column = length // 4 + jnp.arange(channels, dtype=jnp.int32)[None, :]
    phases = ((sample * column) % length).astype(jnp.float32) * (2.0 * math.pi / length)
    stacked = jnp.stack([jnp.cos(phases), -jnp.sin(phases)], axis=2)
    return stacked.reshape(length, 2 * channels).astype(jnp.bfloat16)


def windowed(shaped_volt, prototype, count):
    accumulated = jnp.zeros((shaped_volt.shape[0], count, shaped_volt.shape[2]), jnp.float32)
    for tap_index in range(prototype.shape[0]):
        accumulated = accumulated + prototype[tap_index][None, None, :] * shaped_volt[:, tap_index:tap_index + count, :].astype(jnp.float32)
    return accumulated.astype(jnp.bfloat16)


def spectra_of(shaped_volt, prototype, dft_table, complex_gains, keeping, count):
    frames_win = windowed(shaped_volt, prototype, count)
    raw_spectra = jnp.einsum("nk,ifn->kif", dft_table.astype(jnp.float32), frames_win.astype(jnp.float32))
    channels = dft_table.shape[1] // 2
    local_inputs = shaped_volt.shape[0]
    shaped = raw_spectra.reshape(channels, 2, local_inputs, count)
    gain_parts = complex_gains.T.reshape(channels, 2, local_inputs)[:, :, :, None]
    real_part = gain_parts[:, 0] * shaped[:, 0] - gain_parts[:, 1] * shaped[:, 1]
    imag_part = gain_parts[:, 0] * shaped[:, 1] + gain_parts[:, 1] * shaped[:, 0]
    stacked = jnp.stack([real_part, imag_part], axis=1) * keeping[None, None, :, None]
    return stacked.astype(jnp.bfloat16)


def reference(voltages, prototype, complex_gains, flagged, station_order):
    group_size = 2 * STA_DEV
    groups = INPUTS // group_size
    shaped_volt = voltages.reshape(groups, group_size, FRAMES + TAPS - 1, NFFT)
    gains_grouped = complex_gains.reshape(groups, group_size, 2 * NCHAN)
    keeping = jnp.repeat(1.0 - flagged.astype(jnp.float32), 2).reshape(groups, group_size)
    dft_table = make_table(NFFT, NCHAN)

    def one_group(pieces):
        return spectra_of(pieces[0], prototype, dft_table, pieces[1], pieces[2], FRAMES)

    spectra = lax.map(one_group, (shaped_volt, gains_grouped, keeping))
    spectra = spectra.transpose(1, 2, 0, 3, 4).reshape(NCHAN, 2, INPUTS, FRAMES)
    position = jnp.arange(INPUTS, dtype=jnp.int32)
    source = (2 * station_order[position // 2] + position % 2).astype(jnp.int32)
    ordered = jnp.take(spectra, source, axis=2)

    def one_channel(block_pair):
        left = jnp.concatenate([block_pair[0], block_pair[1]], axis=1)
        lower = jnp.concatenate([-block_pair[1], block_pair[0]], axis=1)
        right = jnp.concatenate([left, lower], axis=0)
        product = jnp.dot(left, right.T, preferred_element_type=jnp.float32) * (1.0 / FRAMES)
        return jnp.stack([product[:, :INPUTS], product[:, INPUTS:]], axis=0).astype(jnp.bfloat16)

    result = lax.map(one_channel, ordered)
    return result.transpose(1, 0, 2, 3)
```

```python
import functools
import math

import jax
import jax.numpy as jnp
import numpy as np
from jax import lax
from jax.experimental import pallas as pl
from jax.experimental.pallas import tpu as pltpu
from jax.sharding import PartitionSpec as P

GROUP = 33
DEPTH = 256
VMEM = pl.BlockSpec(memory_space=pltpu.VMEM)
SMEM = pl.BlockSpec(memory_space=pltpu.SMEM)


def table_rows(length, channels, rows):
    sample = np.arange(length, dtype=np.int64)[None, :]
    column = length // 4 + np.arange(channels, dtype=np.int64)[:, None]
    phases = (sample * column % length) * (2.0 * math.pi / length)
    table = np.zeros((rows, length), np.float32)
    table[:channels] = np.cos(phases)
    table[channels : 2 * channels] = -np.sin(phases)
    return jnp.asarray(table, jnp.bfloat16)


def partner(index, step, size):
    return index ^ step if size & (size - 1) == 0 else (index + step) % size


def slot_of(index, source, size):
    return index ^ source if size & (size - 1) == 0 else (index - source) % size


def channelize(
    me_ref, volt_ref, proto_ref, table_ref, gains_ref, flag_ref, *refs, groups, frames, stride
):
    outs = refs[:groups]
    buf, sems, weights, sums, stage, spectra = refs[groups:]
    inputs = volt_ref.shape[0]
    taps, length = proto_ref.shape
    used = gains_ref.shape[0]
    channels = used // 2
    need = frames + taps - 1
    steps = -(-need // GROUP)

    def fetch(step):
        part = pl.ds(step * GROUP * length, min(GROUP, need - step * GROUP) * length)
        return pltpu.make_async_copy(volt_ref.at[:, part], buf.at[:, part], sems.at[step])

    for step in range(steps):
        fetch(step).start()
    table = table_ref[...].astype(jnp.float32)
    for tap in range(taps):
        weights[tap * stride : (tap + 1) * stride, :] = (
            table * proto_ref[tap : tap + 1, :]
        ).astype(jnp.bfloat16)
    for step in range(steps):
        fetch(step).wait()
        count = min(GROUP, need - step * GROUP)
        total = None
        for low in range(0, length, DEPTH):
            rows = [
                buf[:, (step * GROUP + f) * length + low : (step * GROUP + f) * length + low + DEPTH]
                for f in range(count)
            ]
            part = lax.dot_general(
                jnp.concatenate(rows, axis=0),
                weights[:, low : low + DEPTH],
                (((1,), (1,)), ((), ())),
                preferred_element_type=jnp.float32,
            )
            total = part if total is None else total + part
        sums[step * GROUP : step * GROUP + count] = total.reshape(count, inputs, taps * stride)
    for first in range(0, frames, 16):
        count = min(16, frames - first)
        raw = None
        for tap in range(taps):
            piece = sums[first + tap : first + tap + count, :, tap * stride : tap * stride + used]
            raw = piece if raw is None else raw + piece
        stage[first * inputs : (first + count) * inputs, 0:used] = raw.reshape(count * inputs, used)
    for i in range(inputs):
        raw = stage[pl.ds(i, frames, stride=inputs), :].T[0:used, :]
        real, imag = raw[0:channels], raw[channels:used]
        gain_real = gains_ref[0:channels, i : i + 1]
        gain_imag = gains_ref[channels:used, i : i + 1]
        keep = 1.0 - flag_ref[i // 2].astype(jnp.float32)
        spectra[:, i, 0:frames] = ((gain_real * real - gain_imag * imag) * keep).astype(jnp.bfloat16)
        spectra[:, i, frames:] = ((gain_real * imag + gain_imag * real) * keep).astype(jnp.bfloat16)
    each = channels // groups
    for step in range(groups):
        outs[step][...] = spectra[pl.ds(partner(me_ref[0], step, groups) * each, each)]


def correlate(row_ref, mine_ref, *refs, frames):
    pieces, out_ref, select = refs[:-2], refs[-2], refs[-1]
    blocks, each, local = pieces[0].shape[:3]
    inputs = row_ref.shape[1]
    width = mine_ref.shape[0]
    select[...] = jnp.where(
        lax.broadcasted_iota(jnp.int32, (inputs, inputs), 0) == row_ref[...], 1.0, 0.0
    ).astype(jnp.bfloat16)
    pick = jnp.where(
        lax.broadcasted_iota(jnp.int32, (width, inputs), 1) == mine_ref[...], 1.0, 0.0
    ).astype(jnp.bfloat16)
    for j in range(each):
        columns = jnp.concatenate(
            [piece[b, j] for piece in pieces for b in range(blocks)], axis=0
        )
        picked = jnp.dot(pick, columns, preferred_element_type=jnp.float32).astype(jnp.bfloat16)
        swapped = jnp.concatenate([picked[:, frames:], -picked[:, :frames]], axis=1)
        left = jnp.concatenate([picked, swapped], axis=0)
        product = lax.dot_general(
            left, columns, (((1,), (1,)), ((), ())), preferred_element_type=jnp.float32
        )
        rounded = (product * (1.0 / frames)).astype(jnp.bfloat16)
        ordered = jnp.dot(rounded, select[...], preferred_element_type=jnp.float32)
        ordered = ordered.astype(jnp.bfloat16)
        out_ref[0, j] = ordered[:width]
        out_ref[1, j] = ordered[width:]


def local(voltages, prototype, complex_gains, flagged, station_order):
    inputs = voltages.shape[0]
    taps, length = prototype.shape
    used = complex_gains.shape[1]
    channels = used // 2
    frames = voltages.shape[1] // length - taps + 1
    chan_size = lax.axis_size("chan")
    panel_size = lax.axis_size("panel")
    chan_me = lax.axis_index("chan")
    panel_me = lax.axis_index("panel")
    each = channels // chan_size
    stride = 64 if used <= 64 else -(-used // 128) * 128
    need = frames + taps - 1
    steps = -(-need // GROUP)

    gains = complex_gains.reshape(inputs, channels, 2).transpose(2, 1, 0).reshape(used, inputs)
    spectra = pl.pallas_call(
        functools.partial(channelize, groups=chan_size, frames=frames, stride=stride),
        out_shape=[jax.ShapeDtypeStruct((each, inputs, 2 * frames), jnp.bfloat16)] * chan_size,
        in_specs=[SMEM, pl.BlockSpec(memory_space=pl.ANY), VMEM, VMEM, VMEM, SMEM],
        out_specs=[VMEM] * chan_size,
        scratch_shapes=[
            pltpu.VMEM((inputs, need * length), jnp.bfloat16),
            pltpu.SemaphoreType.DMA((steps,)),
            pltpu.VMEM((taps * stride, length), jnp.bfloat16),
            pltpu.VMEM((need, inputs, taps * stride), jnp.float32),
            pltpu.VMEM((frames * inputs, -(-used // 128) * 128), jnp.float32),
            pltpu.VMEM((channels, inputs, 2 * frames), jnp.bfloat16),
        ],
        compiler_params=pltpu.CompilerParams(vmem_limit_bytes=56 * 1024 * 1024),
        name="channelize",
    )(
        chan_me[None].astype(jnp.int32),
        voltages,
        prototype,
        table_rows(length, channels, stride),
        gains,
        flagged,
    )

    turned = [spectra[0]]
    for step in range(1, chan_size):
        pairs = [(i, partner(i, step, chan_size)) for i in range(chan_size)]
        turned.append(lax.ppermute(spectra[step], "chan", pairs))
    turned = jnp.stack(turned)

    cores = 2 if panel_size % 2 == 0 else 1
    chips = panel_size // cores
    pieces = [turned]
    for step in range(1, chips):
        pairs = [
            (i * cores + k, partner(i, step, chips) * cores + k)
            for i in range(chips)
            for k in range(cores)
        ]
        pieces.append(lax.ppermute(turned, "panel", pairs))
    if cores == 2:
        swap = [(i, i ^ 1) for i in range(panel_size)]
        pieces += [lax.ppermute(piece, "panel", swap) for piece in pieces]

    inputs_all = 2 * station_order.shape[0]
    width = inputs_all // panel_size
    source = (2 * station_order[:, None] + jnp.arange(2, dtype=jnp.int32)[None, :]).reshape(-1)
    device = source // inputs
    chan_from, panel_from = device // panel_size, device % panel_size
    piece = slot_of(panel_me % cores, panel_from % cores, cores) * chips + slot_of(
        panel_me // cores, panel_from // cores, chips
    )
    row = (
        piece * (chan_size * inputs)
        + slot_of(chan_me, chan_from, chan_size) * inputs
        + source % inputs
    )
    mine = lax.dynamic_slice_in_dim(row, panel_me * width, width)

    return pl.pallas_call(
        functools.partial(correlate, frames=frames),
        out_shape=jax.ShapeDtypeStruct((2, each, width, inputs_all), jnp.bfloat16),
        in_specs=[VMEM] * (2 + len(pieces)),
        out_specs=VMEM,
        scratch_shapes=[pltpu.VMEM((inputs_all, inputs_all), jnp.bfloat16)],
        compiler_params=pltpu.CompilerParams(vmem_limit_bytes=56 * 1024 * 1024),
        name="correlate",
    )(row[None, :], mine[:, None], *pieces)


def solution(mesh):
    placed = (
        P(("chan", "panel"), None),
        P(),
        P(("chan", "panel"), None),
        P(("chan", "panel")),
        P(),
    )
    return jax.shard_map(
        local, mesh=mesh, in_specs=placed, out_specs=P(None, "chan", "panel", None), check_vma=False
    )
```

```python
import functools
import math

import jax
import jax.numpy as jnp
import numpy as np
from jax import lax
from jax.experimental import pallas as pl
from jax.experimental.pallas import tpu as pltpu
from jax.sharding import PartitionSpec as P

GROUP = 33
PART = 11
CHANNELIZE_MIB = 40
CORRELATE_MIB = 40
VMEM = pl.BlockSpec(memory_space=pltpu.VMEM)
SMEM = pl.BlockSpec(memory_space=pltpu.SMEM)


def table_rows(length, channels, rows):
    sample = np.arange(length, dtype=np.int64)[None, :]
    column = length // 4 + np.arange(channels, dtype=np.int64)[:, None]
    phases = (sample * column % length) * (2.0 * math.pi / length)
    table = np.zeros((rows, length), np.float32)
    table[:channels] = np.cos(phases)
    table[channels : 2 * channels] = -np.sin(phases)
    return jnp.asarray(table, jnp.bfloat16)


def partner(index, step, size):
    return index ^ step if size & (size - 1) == 0 else (index + step) % size


def slot_of(index, source, size):
    return index ^ source if size & (size - 1) == 0 else (index - source) % size


def channelize(
    volt_ref, proto_ref, table_ref, gains_ref, flag_ref, *refs, groups, frames, stride
):
    outs = refs[:groups]
    buf, sems, flags, proto, table, given, weights, sums, stage, gains, spectra = refs[groups:]
    inputs = volt_ref.shape[0]
    taps, length = proto_ref.shape
    used = gains_ref.shape[1]
    channels = used // 2
    need = frames + taps - 1
    parts = -(-need // PART)

    copies = [
        pltpu.make_async_copy(source, target, sems.at[parts + k])
        for k, (source, target) in enumerate(
            ((proto_ref, proto), (table_ref, table), (gains_ref, given), (flag_ref, flags))
        )
    ]
    for part in range(parts):
        span = pl.ds(part * PART * length, min(PART, need - part * PART) * length)
        copies.append(
            pltpu.make_async_copy(volt_ref.at[:, span], buf.at[:, span], sems.at[part])
        )
    for copy in copies:
        copy.start()
    for copy in copies[:4]:
        copy.wait()
    gains[0:inputs, 0:used] = given[...]
    gains[...] = gains[...].T
    cosines = table[...].astype(jnp.float32)
    for tap in range(taps):
        weights[tap * stride : (tap + 1) * stride, :] = (
            cosines * proto[tap : tap + 1, :]
        ).astype(jnp.bfloat16)
    for copy in copies[4:]:
        copy.wait()
    done = 0
    for low in range(0, need, GROUP):
        count = min(GROUP, need - low)
        rows = [buf[:, (low + f) * length : (low + f + 1) * length] for f in range(count)]
        total = lax.dot_general(
            jnp.concatenate(rows, axis=0),
            weights[...],
            (((1,), (1,)), ((), ())),
            preferred_element_type=jnp.float32,
        )
        sums[low : low + count] = total.reshape(count, inputs, taps * stride)
        ready = low + count - taps + 1
        while done < ready:
            size = min(16, ready - done)
            raw = None
            for tap in range(taps):
                piece = sums[done + tap : done + tap + size, :, tap * stride : tap * stride + used]
                raw = piece if raw is None else raw + piece
            stage[done * inputs : (done + size) * inputs, 0:used] = raw.reshape(size * inputs, used)
            done += size
    gains_real = gains[pl.ds(0, channels, stride=2), :]
    gains_imag = gains[pl.ds(1, channels, stride=2), :]
    for i in range(inputs):
        raw = stage[pl.ds(i, frames, stride=inputs), :].T[0:used, :]
        real, imag = raw[0:channels], raw[channels:used]
        gain_real, gain_imag = gains_real[:, i : i + 1], gains_imag[:, i : i + 1]
        keep = 1.0 - flags[i // 2].astype(jnp.float32)
        spectra[:, i, 0:frames] = ((gain_real * real - gain_imag * imag) * keep).astype(jnp.bfloat16)
        spectra[:, i, frames:] = ((gain_real * imag + gain_imag * real) * keep).astype(jnp.bfloat16)
    each = channels // groups
    me = lax.axis_index("chan")
    for step in range(groups):
        outs[step][...] = spectra[pl.ds(partner(me, step, groups) * each, each)]


def correlate(row_ref, mine_ref, *refs, frames):
    pieces, out_ref, select = refs[:-2], refs[-2], refs[-1]
    blocks, each, local = pieces[0].shape[:3]
    inputs = row_ref.shape[1]
    width = mine_ref.shape[0]
    select[...] = jnp.where(
        lax.broadcasted_iota(jnp.int32, (inputs, inputs), 0) == row_ref[...], 1.0, 0.0
    ).astype(jnp.bfloat16)
    pick = jnp.where(
        lax.broadcasted_iota(jnp.int32, (width, inputs), 1) == mine_ref[...], 1.0, 0.0
    ).astype(jnp.bfloat16)
    for j in range(each):
        columns = jnp.concatenate(
            [piece[b, j] for piece in pieces for b in range(blocks)], axis=0
        )
        picked = jnp.dot(pick, columns, preferred_element_type=jnp.float32).astype(jnp.bfloat16)
        swapped = jnp.concatenate([picked[:, frames:], -picked[:, :frames]], axis=1)
        left = jnp.concatenate([picked, swapped], axis=0)
        product = lax.dot_general(
            left, columns, (((1,), (1,)), ((), ())), preferred_element_type=jnp.float32
        )
        rounded = (product * (1.0 / frames)).astype(jnp.bfloat16)
        ordered = jnp.dot(rounded, select[...], preferred_element_type=jnp.float32)
        ordered = ordered.astype(jnp.bfloat16)
        out_ref[0, j] = ordered[:width]
        out_ref[1, j] = ordered[width:]


def local(voltages, prototype, complex_gains, flagged, station_order):
    inputs = voltages.shape[0]
    taps, length = prototype.shape
    used = complex_gains.shape[1]
    channels = used // 2
    frames = voltages.shape[1] // length - taps + 1
    chan_size = lax.axis_size("chan")
    panel_size = lax.axis_size("panel")
    chan_me = lax.axis_index("chan")
    panel_me = lax.axis_index("panel")
    each = channels // chan_size
    stride = 64 if used <= 64 else -(-used // 128) * 128
    need = frames + taps - 1
    lanes = -(-used // 128) * 128
    in_hbm = pl.BlockSpec(memory_space=pltpu.HBM)

    scratch = [
        ((inputs, need * length), jnp.bfloat16),
        ((taps, length), jnp.float32),
        ((stride, length), jnp.bfloat16),
        ((inputs, used), jnp.float32),
        ((taps * stride, length), jnp.bfloat16),
        ((need, inputs, taps * stride), jnp.float32),
        ((frames * inputs, lanes), jnp.float32),
        ((lanes, lanes), jnp.float32),
        ((channels, inputs, 2 * frames), jnp.bfloat16),
    ]
    scratch = [pltpu.VMEM(shape, dtype) for shape, dtype in scratch]
    scratch[1:1] = [
        pltpu.SemaphoreType.DMA((-(-need // PART) + 4,)),
        pltpu.SMEM(flagged.shape, jnp.int32),
    ]
    spectra = pl.pallas_call(
        functools.partial(channelize, groups=chan_size, frames=frames, stride=stride),
        out_shape=[jax.ShapeDtypeStruct((each, inputs, 2 * frames), jnp.bfloat16)] * chan_size,
        in_specs=[in_hbm] * 5,
        out_specs=[VMEM] * chan_size,
        scratch_shapes=scratch,
        compiler_params=pltpu.CompilerParams(vmem_limit_bytes=CHANNELIZE_MIB * 1024 * 1024),
        name="channelize",
    )(
        *(
            pltpu.with_memory_space_constraint(operand, pltpu.HBM)
            for operand in (
                voltages,
                prototype,
                table_rows(length, channels, stride),
                complex_gains,
                flagged,
            )
        )
    )

    turned = [spectra[0]]
    for step in range(1, chan_size):
        pairs = [(i, partner(i, step, chan_size)) for i in range(chan_size)]
        turned.append(lax.ppermute(spectra[step], "chan", pairs))
    turned = jnp.stack(turned)

    cores = 2 if panel_size % 2 == 0 else 1
    chips = panel_size // cores
    pieces = [turned]
    for step in range(1, chips):
        pairs = [
            (i * cores + k, partner(i, step, chips) * cores + k)
            for i in range(chips)
            for k in range(cores)
        ]
        pieces.append(lax.ppermute(turned, "panel", pairs))
    if cores == 2:
        swap = [(i, i ^ 1) for i in range(panel_size)]
        pieces += [lax.ppermute(piece, "panel", swap) for piece in pieces]

    inputs_all = 2 * station_order.shape[0]
    width = inputs_all // panel_size
    source = (2 * station_order[:, None] + jnp.arange(2, dtype=jnp.int32)[None, :]).reshape(-1)
    device = source // inputs
    chan_from, panel_from = device // panel_size, device % panel_size
    piece = slot_of(panel_me % cores, panel_from % cores, cores) * chips + slot_of(
        panel_me // cores, panel_from // cores, chips
    )
    row = (
        piece * (chan_size * inputs)
        + slot_of(chan_me, chan_from, chan_size) * inputs
        + source % inputs
    )
    mine = lax.dynamic_slice_in_dim(row, panel_me * width, width)

    return pl.pallas_call(
        functools.partial(correlate, frames=frames),
        out_shape=jax.ShapeDtypeStruct((2, each, width, inputs_all), jnp.bfloat16),
        in_specs=[VMEM] * (2 + len(pieces)),
        out_specs=VMEM,
        scratch_shapes=[pltpu.VMEM((inputs_all, inputs_all), jnp.bfloat16)],
        compiler_params=pltpu.CompilerParams(vmem_limit_bytes=CORRELATE_MIB * 1024 * 1024),
        name="correlate",
    )(row[None, :], mine[:, None], *pieces)


def solution(mesh):
    placed = (
        P(("chan", "panel"), None),
        P(),
        P(("chan", "panel"), None),
        P(("chan", "panel")),
        P(),
    )
    return jax.shard_map(
        local, mesh=mesh, in_specs=placed, out_specs=P(None, "chan", "panel", None), check_vma=False
    )
```

```python
import functools
import math

import jax
import jax.numpy as jnp
import numpy as np
from jax import lax
from jax.experimental import pallas as pl
from jax.experimental.pallas import tpu as pltpu
from jax.sharding import PartitionSpec as P

STEPS = 4
LEAD = 1
SMALL = 1024
CHANNELIZE_MIB = 40
CORRELATE_MIB = 40
VMEM = pl.BlockSpec(memory_space=pltpu.VMEM)
SMEM = pl.BlockSpec(memory_space=pltpu.SMEM)


def table_rows(length, channels, rows):
    sample = np.arange(length, dtype=np.int64)[None, :]
    column = length // 4 + np.arange(channels, dtype=np.int64)[:, None]
    phases = (sample * column % length) * (2.0 * math.pi / length)
    table = np.zeros((rows, length), np.float32)
    table[:channels] = np.cos(phases)
    table[channels : 2 * channels] = -np.sin(phases)
    return jnp.asarray(table, jnp.bfloat16)


def partner(index, step, size):
    return index ^ step if size & (size - 1) == 0 else (index + step) % size


def slot_of(index, source, size):
    return index ^ source if size & (size - 1) == 0 else (index - source) % size


def channelize(
    volt_ref, proto_ref, table_ref, gains_ref, flag_ref, *refs, groups, frames, stride
):
    outs = refs[:groups]
    buf, sems, flags, proto, table, given, weights, sums, stage, gains, tail = refs[groups:]
    inputs = volt_ref.shape[0]
    taps, length = proto_ref.shape
    used = gains_ref.shape[1]
    channels = used // 2
    need = frames + taps - 1
    parts = STEPS
    group = -(-need // parts)

    copies = [
        pltpu.make_async_copy(source, target, sems.at[parts + k])
        for k, (source, target) in enumerate(
            ((proto_ref, proto), (table_ref, table), (gains_ref, given), (flag_ref, flags))
        )
    ]
    for part in range(parts):
        span = pl.ds(part * group * length, min(group, need - part * group) * length)
        copies.append(
            pltpu.make_async_copy(volt_ref.at[:, span], buf.at[:, span], sems.at[part])
        )
    for copy in copies:
        copy.start()
    for copy in copies[:4]:
        copy.wait()
    gains[0:inputs, 0:used] = given[...]
    gains[...] = gains[...].T
    cosines = table[...].astype(jnp.float32)
    for tap in range(taps):
        weights[tap * stride : (tap + 1) * stride, :] = (
            cosines * proto[tap : tap + 1, :]
        ).astype(jnp.bfloat16)
    for copy in copies[4 : 4 + LEAD]:
        copy.wait()

    def step(index, carry):
        for part in range(LEAD, parts):
            pl.when(index == part)(copies[4 + part].wait)
        low = index * group
        rows = [
            buf[:, pl.ds(pl.multiple_of((low + f) * length, length), length)] for f in range(group)
        ]
        total = lax.dot_general(
            jnp.concatenate(rows, axis=0),
            weights[...],
            (((1,), (1,)), ((), ())),
            preferred_element_type=jnp.float32,
        )
        sums[pl.ds(low, group)] = total.reshape(group, inputs, taps * stride)
        first = jnp.maximum(low - taps + 1, 0)
        for lag in range(0, group, 11):
            size = min(11, group - lag)
            raw = None
            for tap in range(taps):
                piece = sums[
                    pl.ds(first + lag + tap, size), :, tap * stride : tap * stride + used
                ]
                raw = piece if raw is None else raw + piece
            target = pl.ds(pl.multiple_of((first + lag) * inputs, inputs), size * inputs)
            stage[target, 0:used] = raw.reshape(size * inputs, used)
        return carry

    lax.fori_loop(0, parts, step, 0)
    lanes = gains.shape[1]
    gains_real = gains[pl.ds(0, channels, stride=2), :]
    gains_imag = gains[pl.ds(1, channels, stride=2), :]

    def finish(half, carry):
        base = half * 8
        shift = lax.rem(lanes - base, lanes)
        rolled_real = pltpu.roll(gains_real, shift, 1)
        rolled_imag = pltpu.roll(gains_imag, shift, 1)
        for k in range(8):
            raw = stage[pl.ds(base + k, frames, stride=inputs), :].T[0:used, :]
            real, imag = raw[0:channels], raw[channels:used]
            gain_real, gain_imag = rolled_real[:, k : k + 1], rolled_imag[:, k : k + 1]
            keep = 1.0 - flags[half * 4 + k // 2].astype(jnp.float32)
            tail[half, :, k, 0:frames] = (gain_real * real - gain_imag * imag) * keep
            tail[half, :, k, frames:] = (gain_real * imag + gain_imag * real) * keep
        return carry

    lax.fori_loop(0, inputs // 8, finish, 0)
    each = channels // groups
    me = lax.axis_index("chan")
    for step in range(groups):
        start = partner(me, step, groups) * each
        halves = [tail[half, pl.ds(start, each)] for half in range(inputs // 8)]
        outs[step][...] = jnp.concatenate(halves, axis=1).astype(jnp.bfloat16)


def correlate(row_ref, mine_ref, *refs, frames):
    pieces, out_ref, select, products = refs[:-3], refs[-3], refs[-2], refs[-1]
    each = pieces[0].shape[1]
    inputs = row_ref.shape[1]
    width = mine_ref.shape[0]
    batch = each if inputs <= SMALL else 1
    select[...] = jnp.where(
        lax.broadcasted_iota(jnp.int32, (inputs, inputs), 0) == row_ref[...], 1.0, 0.0
    ).astype(jnp.bfloat16)
    pick = jnp.where(
        lax.broadcasted_iota(jnp.int32, (width, inputs), 1) == mine_ref[...], 1.0, 0.0
    ).astype(jnp.bfloat16)

    def channel(j, carry):
        columns = jnp.concatenate(
            [piece[b, j] for piece in pieces for b in range(piece.shape[0])], axis=0
        )
        picked = jnp.dot(pick, columns, preferred_element_type=jnp.float32).astype(jnp.bfloat16)
        swapped = jnp.concatenate([picked[:, frames:], -picked[:, :frames]], axis=1)
        left = jnp.concatenate([picked, swapped], axis=0)
        product = lax.dot_general(
            left, columns, (((1,), (1,)), ((), ())), preferred_element_type=jnp.float32
        )
        rows = pl.ds(pl.multiple_of(j * 2 * width, 2 * width), 2 * width)
        products[rows, :] = (product * (1.0 / frames)).astype(jnp.bfloat16)
        return carry

    lax.fori_loop(0, each, channel, 0, unroll=batch)

    def reorder(k, carry):
        rows = pl.ds(pl.multiple_of(k * batch * 2 * width, 2 * width), batch * 2 * width)
        ordered = jnp.dot(products[rows, :], select[...], preferred_element_type=jnp.float32)
        ordered = ordered.astype(jnp.bfloat16).reshape(batch, 2, width, inputs)
        for i in range(batch):
            out_ref[0, k * batch + i] = ordered[i, 0]
            out_ref[1, k * batch + i] = ordered[i, 1]
        return carry

    lax.fori_loop(0, each // batch, reorder, 0)


def local(voltages, prototype, complex_gains, flagged, station_order):
    inputs = voltages.shape[0]
    taps, length = prototype.shape
    used = complex_gains.shape[1]
    channels = used // 2
    frames = voltages.shape[1] // length - taps + 1
    chan_size = lax.axis_size("chan")
    panel_size = lax.axis_size("panel")
    chan_me = lax.axis_index("chan")
    panel_me = lax.axis_index("panel")
    each = channels // chan_size
    stride = 64 if used <= 64 else -(-used // 128) * 128
    need = frames + taps - 1
    padded = -(-need // STEPS) * STEPS
    lanes = -(-used // 128) * 128
    in_hbm = pl.BlockSpec(memory_space=pltpu.HBM)

    scratch = [
        ((inputs, padded * length), jnp.bfloat16),
        ((taps, length), jnp.float32),
        ((stride, length), jnp.bfloat16),
        ((inputs, used), jnp.float32),
        ((taps * stride, length), jnp.bfloat16),
        ((padded + taps, inputs, taps * stride), jnp.float32),
        (((padded + taps) * inputs, lanes), jnp.float32),
        ((lanes, lanes), jnp.float32),
        ((inputs // 8, channels, 8, 2 * frames), jnp.float32),
    ]
    scratch = [pltpu.VMEM(shape, dtype) for shape, dtype in scratch]
    scratch[1:1] = [
        pltpu.SemaphoreType.DMA((STEPS + 4,)),
        pltpu.SMEM(flagged.shape, jnp.int32),
    ]
    spectra = pl.pallas_call(
        functools.partial(channelize, groups=chan_size, frames=frames, stride=stride),
        out_shape=[jax.ShapeDtypeStruct((each, inputs, 2 * frames), jnp.bfloat16)] * chan_size,
        in_specs=[in_hbm] * 5,
        out_specs=[VMEM] * chan_size,
        scratch_shapes=scratch,
        compiler_params=pltpu.CompilerParams(vmem_limit_bytes=CHANNELIZE_MIB * 1024 * 1024),
        name="channelize",
    )(
        *(
            pltpu.with_memory_space_constraint(operand, pltpu.HBM)
            for operand in (
                voltages,
                prototype,
                table_rows(length, channels, stride),
                complex_gains,
                flagged,
            )
        )
    )

    own = spectra[0][None]
    rest = []
    for step in range(1, chan_size):
        pairs = [(i, partner(i, step, chan_size)) for i in range(chan_size)]
        rest.append(lax.ppermute(spectra[step], "chan", pairs))
    rest = jnp.stack(rest)

    cores = 2 if panel_size % 2 == 0 else 1
    chips = panel_size // cores

    def along(shard, step):
        pairs = [
            (i * cores + k, partner(i, step, chips) * cores + k)
            for i in range(chips)
            for k in range(cores)
        ]
        return lax.ppermute(shard, "panel", pairs)

    shards = [(own, rest)]
    shards += [(along(own, step), along(rest, step)) for step in range(1, chips)]
    if cores == 2:
        swap = [(i, i ^ 1) for i in range(panel_size)]
        shards += [tuple(lax.ppermute(part, "panel", swap) for part in shard) for shard in shards]
    pieces = [part for shard in shards for part in shard]

    inputs_all = 2 * station_order.shape[0]
    width = inputs_all // panel_size
    source = (2 * station_order[:, None] + jnp.arange(2, dtype=jnp.int32)[None, :]).reshape(-1)
    device = source // inputs
    chan_from, panel_from = device // panel_size, device % panel_size
    piece = slot_of(panel_me % cores, panel_from % cores, cores) * chips + slot_of(
        panel_me // cores, panel_from // cores, chips
    )
    row = (
        piece * (chan_size * inputs)
        + slot_of(chan_me, chan_from, chan_size) * inputs
        + source % inputs
    )
    mine = lax.dynamic_slice_in_dim(row, panel_me * width, width)

    return pl.pallas_call(
        functools.partial(correlate, frames=frames),
        out_shape=jax.ShapeDtypeStruct((2, each, width, inputs_all), jnp.bfloat16),
        in_specs=[VMEM] * (2 + len(pieces)),
        out_specs=VMEM,
        scratch_shapes=[
            pltpu.VMEM((inputs_all, inputs_all), jnp.bfloat16),
            pltpu.VMEM((each * 2 * width, inputs_all), jnp.bfloat16),
        ],
        compiler_params=pltpu.CompilerParams(vmem_limit_bytes=CORRELATE_MIB * 1024 * 1024),
        name="correlate",
    )(row[None, :], mine[:, None], *pieces)


def solution(mesh):
    placed = (
        P(("chan", "panel"), None),
        P(),
        P(("chan", "panel"), None),
        P(("chan", "panel")),
        P(),
    )
    return jax.shard_map(
        local, mesh=mesh, in_specs=placed, out_specs=P(None, "chan", "panel", None), check_vma=False
    )
```
